32 devices in a mesh: tm: 4 (over y, x), space: 8 (over z, core).
Axes of the slice: x: 2, y: 2, z: 4, core: 2. Of those that a mesh axis runs over, the one named last changes fastest.
Arguments:
- starts: float32 [4, 8192, 128], P('tm', 'space'), may hold values from -6 to 6
- volume_op: float32 [128, 128], replicated, may hold values from -0.1875 to 0.1875
- face_lifts: float32 [6, 128, 128], replicated, may hold values from -0.1875 to 0.1875
- neighbours: int32 [8192, 6], P('space'), may hold values from 0 to 8191, as said below
- orientation: int32 [8192, 6], P('space'), may hold values from 0 to 3
Outputs:
- updated: float32 [4, 8192, 128], P('tm', 'space')
The draws below stay inside these ranges and needn't reach their ends.
Inputs may be any that keep to these rules, and one draw needn't show every extreme that they name: neighbours[e, f] lies at most 128 elements from e in the periodic element order, that is it equals (e + k) mod 8192 with -128 <= k <= 128; both k = 128 and k = -128 occur.
All inputs are finite; a program needn't handle non-finite values.
Results may differ from the reference program's by a relative error of at most 0.0001.
Values sent between devices are 32-bit elements; how exact they have to be, the bound alone decides.
A program may use at most 64 MiB of HBM per device.

```python
import jax
import jax.numpy as jnp
from jax import lax

NODES = 128
REACH = 128
STEPS = 4
SLICES = 4
ELEMS = 8192


def draw_neighbours(key, part):
    offsets = jax.random.randint(key, (ELEMS, 6), -REACH, REACH + 1, dtype=jnp.int32)
    row_index = jnp.arange(ELEMS, dtype=jnp.int32)
    at_edge = row_index % 8 == 0
    offsets = offsets.at[:, 0].set(jnp.where(at_edge, REACH, offsets[:, 0]))
    offsets = offsets.at[:, 1].set(jnp.where(at_edge, -REACH, offsets[:, 1]))
    offsets = offsets.at[:, 2].set(jnp.where(row_index % 8 >= 6, 1, offsets[:, 2]))
    return ((row_index[:, None] + offsets) % ELEMS).astype(jnp.int32)


def place_ends(entries, stream_key, smallest, largest):
    dims = entries.shape
    index_at = [jax.random.randint(jax.random.fold_in(stream_key, axis), (), 0, dims[axis]) for axis in range(len(dims))]
    entries = entries.at[tuple(index_at)].set(smallest)
    longest = dims.index(max(dims))
    index_at[longest] = (index_at[longest] + 1) % dims[longest]
    return entries.at[tuple(index_at)].set(largest)


def block_scale(key, dims, shards, least, top_value):
    level = 1.0
    for position, parts in shards:
        heights = jax.random.uniform(jax.random.fold_in(jax.random.fold_in(key, 6), position), (parts,), jnp.float32, least / len(shards), top_value / len(shards))
        level = level * jnp.repeat(jnp.exp(heights), dims[position] // parts).reshape((-1,) + (1,) * (len(dims) - 1 - position))
    return level


def bell_draw(key, shape, scale, reach, shards=(), kind=jnp.bfloat16):
    result = scale * jax.random.normal(key, shape, jnp.float32)
    if shards:
        result = result * block_scale(key, shape, shards, -0.22, 0.18)
    return jnp.clip(result, -reach, reach).astype(kind)


def setup_inputs(seed: int = 0) -> dict:
    key_of = jax.random.split(jax.random.key(seed), 6)
    starts = bell_draw(key_of[0], (SLICES, ELEMS, NODES), 1.0, 6.0, ((0, 4), (1, 8)), jnp.float32)
    volume_op = bell_draw(key_of[1], (NODES, NODES), (7 * NODES) ** -0.5, 0.1875, (), jnp.float32)
    face_lifts = bell_draw(key_of[2], (6, NODES, NODES), (7 * NODES) ** -0.5, 0.1875, (), jnp.float32)
    neighbours = draw_neighbours(jax.random.fold_in(key_of[5], 71), 0)
    orientation = place_ends(jax.random.randint(key_of[4], (ELEMS, 6), 0, 4), jax.random.fold_in(key_of[4], 1), 0, 3).astype(jnp.int32)
    return {"starts": starts, "volume_op": volume_op, "face_lifts": face_lifts, "neighbours": neighbours, "orientation": orientation}


FINE_DT = 0.25
COARSE_DT = 1.0


def twist_rows(gathered, orient_ids):
    node_count = gathered.shape[-1]
    flipped = jnp.where((orient_ids % 2 == 1)[..., None], gathered[..., ::-1], gathered)
    return jnp.where((orient_ids // 2 == 1)[..., None], jnp.roll(flipped, node_count // 2, axis=-1), flipped)


def operate(center, extended, places, orient_ids, volume_op, face_lifts):
    elem_count, node_count = center.shape
    faces = twist_rows(extended[places], orient_ids).reshape(elem_count, 6 * node_count)
    flux = jnp.dot(faces, face_lifts.reshape(6 * node_count, node_count), precision=lax.Precision.HIGHEST, preferred_element_type=jnp.float32)
    inner = jnp.dot(center, volume_op, precision=lax.Precision.HIGHEST, preferred_element_type=jnp.float32)
    return inner + flux - center


def reference(starts, volume_op, face_lifts, neighbours, orientation):
    def coarse_map(state):
        return state + COARSE_DT * operate(state, state, neighbours, orientation, volume_op, face_lifts)

    results = []
    previous = None
    for slot_id in range(SLICES):
        fine_state = starts[slot_id]
        for step_idx in range(STEPS):
            fine_state = fine_state + FINE_DT * operate(fine_state, fine_state, neighbours, orientation, volume_op, face_lifts)
        if slot_id == 0:
            current = fine_state
        else:
            current = coarse_map(previous) + (fine_state - coarse_map(starts[slot_id]))
        results.append(current)
        previous = current
    return jnp.stack(results)
```

```python
import functools

import jax
import jax.numpy as jnp
import numpy as np
from jax import lax
from jax.experimental import pallas as pl
from jax.experimental.pallas import tpu as pltpu
from jax.sharding import PartitionSpec as P

REACH = 128
STEPS = 4
FACES = 6
BLOCK = 256
WINDOW = BLOCK + 2 * REACH

FINE = [81 / 256, 108 / 256, 54 / 256, 12 / 256, 1 / 256]
DIFF = [81 / 256, -148 / 256, 54 / 256, 12 / 256, 1 / 256]

MESH = pl.DeviceIdType.MESH
F32 = jnp.float32
BF16 = jnp.bfloat16


def twist_basis(nodes):
    quarter = nodes // 4
    basis = np.zeros((nodes, nodes), np.float32)
    for column in range(nodes):
        kind, rep = divmod(column, quarter)
        flip, turn = kind & 1, kind >> 1
        half = nodes // 2
        for a in range(2):
            for b in range(2):
                row = nodes - 1 - rep if a else rep
                row = (row + half) % nodes if b else row
                basis[row, column] = 0.5 * (-1) ** (flip * a + turn * b)
    return basis


def split(x):
    hi = x.astype(BF16)
    return hi, (x - hi.astype(F32)).astype(BF16)


def pair(x):
    return jnp.concatenate(split(x), axis=-1)


def kernel(
    times, ring, starts, volume, lifts, nbr, orient, basis_t, out,
    got, coded, state, halves, hot, place, signs, wide, low, out_edge, in_edge,
    s_send, s_recv, e_send, e_recv,
):
    rows, nodes = starts.shape[1], starts.shape[2]
    blocks, tiles = rows // BLOCK, rows // REACH
    n = lax.axis_index("tm")
    me = lax.axis_index("space")
    right, left = lax.rem(me + 1, ring), lax.rem(me + ring - 1, ring)

    barrier = pltpu.get_barrier_semaphore()
    for side in (left, right):
        pl.semaphore_signal(barrier, inc=1, device_id={"space": side}, device_id_type=MESH)
    for step in range(1, times):
        pl.semaphore_signal(
            barrier, inc=1, device_id={"tm": lax.rem(n + step, times)}, device_id_type=MESH
        )
    pl.semaphore_wait(barrier, times + 1)

    order = list(range(1, blocks - 1)) + [0, blocks - 1]
    square = times == 4 and blocks == 4

    def rows_of(b):
        return pl.ds(pl.multiple_of(b * BLOCK, BLOCK), BLOCK)

    def send(source, b, target, own):
        held = starts.at[0] if own else got.at[source]
        return pltpu.make_async_remote_copy(
            src_ref=held.at[rows_of(b)],
            dst_ref=got.at[source, rows_of(b)],
            send_sem=s_send.at[target, source, b],
            recv_sem=s_recv.at[source, b],
            device_id={"tm": target},
            device_id_type=MESH,
        )

    own_hops, passed_hops = [], []
    if square:
        for b in range(blocks):
            own_hops += [(0, 0, b, 1), (0, 0, b, 2), (1, 1, b, 3), (2, 2, b, 3)]
            passed_hops += [(1 if b < 2 else 2, 0, b, 3), (3, 1, b, 2)]
        first = [(0, 1, 0), (2, 2, 0), (1, 1, 0), (3, 2, 0), (2, 1, 0), (0, 2, 0), (3, 1, 0), (1, 2, 0)]

        @pl.when(n == 0)
        def _():
            for b, target, source in first:
                send(source, b, target, True).start()

        for early in (1, 2):

            @pl.when(n == early)
            def _():
                send(early, order[0], 3, True).start()
    else:
        for target in range(times - 1, 0, -1):

            @pl.when(n < target)
            def _():
                for b in order:
                    send(n, b, target, True).start()

    turn_in = basis_t[...].astype(BF16)
    turn_in = jnp.concatenate([turn_in, turn_in], axis=1)

    def rotate(x):
        return lax.dot_general(turn_in, pair(x), (((1,), (1,)), ((), ())), preferred_element_type=F32)

    def operator(a):
        return split(rotate(jnp.dot(turn_in, jnp.concatenate(split(a), axis=0), preferred_element_type=F32)))

    for p in range(FACES // 2):
        h0, l0 = operator(lifts[2 * p])
        h1, l1 = operator(lifts[2 * p + 1])
        high = jnp.concatenate([h0, h1], axis=1)
        wide[p] = jnp.concatenate([high, jnp.concatenate([l0, l1], axis=1)], axis=0)
        low[p] = high
    hv, lv = operator(volume[...])
    wide[FACES // 2] = jnp.concatenate(
        [jnp.concatenate([hv, hv], axis=1), jnp.concatenate([lv, lv], axis=1)], axis=0
    )

    total = rows * ring
    lane = lax.broadcasted_iota(jnp.int32, (FACES, REACH), 1)
    for t in range(tiles):
        at = pl.ds(t * REACH, REACH)
        offset = nbr[:, at] - (me * rows + t * REACH + lane)
        offset = jnp.where(offset > REACH, offset - total, offset)
        offset = jnp.where(offset < -REACH, offset + total, offset)
        place[t] = lane + REACH + offset
        o = orient[:, at]
        signs[t, 0] = (1 - 2 * (o % 2)).astype(F32)
        signs[t, 1] = (1 - 2 * (o // 2)).astype(F32)

    column = lax.broadcasted_iota(jnp.int32, (WINDOW, BLOCK), 0)
    for b in range(blocks):
        for p in range(FACES // 2):
            f = pl.ds(2 * p + 1, 1)
            row = jnp.concatenate([place[2 * b, f, :], place[2 * b + 1, f, :] + REACH], axis=1)
            hot[b, p] = jnp.where(column == row, 1.0, 0.0).astype(BF16)

    for b in range(blocks):
        coded[n, b] = rotate(starts[0, rows_of(b), :])

    def arrive(j, b):
        send(j, b, n, False).wait_recv()
        coded[j, b] = rotate(got[j, rows_of(b), :])

    @pl.when(n > 0)
    def _():
        def body(i, carry):
            b = lax.rem(i + jnp.where(n == 2, blocks // 2, 0), blocks)
            send(0, b, n, False).wait_recv()
            if square:

                @pl.when(jnp.logical_and(n < 3, i < 2))
                def _():
                    send(0, b, 3, False).start()

            coded[0, b] = rotate(got[0, rows_of(b), :])
            return carry

        lax.fori_loop(0, blocks, body, 0)

    if square:
        for later in (1, 2):

            @pl.when(n == later)
            def _():
                for b in order[1:]:
                    send(later, b, 3, True).start()

    def forcing(step, b):
        acc = None
        for i in range(STEPS + 1):
            j = step - STEPS + i
            coef = jnp.where(j == 0, FINE[i], DIFF[i]).astype(F32)
            held = jnp.logical_and(j >= 0, j <= n)
            if i == STEPS:
                held = jnp.logical_and(held, jnp.logical_or(step >= n, step == 0))
            place_of = jnp.where(held, j, n)
            term = jnp.where(held, coef, 0.0) * coded[place_of, b]
            acc = term if acc is None else acc + term
        return acc

    def edge_copy(step, side):
        return pltpu.make_async_remote_copy(
            src_ref=out_edge.at[step, side],
            dst_ref=in_edge.at[step, 1 - side],
            send_sem=e_send.at[step, side],
            recv_sem=e_recv.at[step, 1 - side],
            device_id={"space": right if side else left},
            device_id_type=MESH,
        )

    last = n + STEPS

    def store(slot, b, y):
        both = jnp.concatenate(split(y), axis=0)
        for u in range(2):
            state[slot, 2 * b + 1 + u] = y[:, u * REACH : (u + 1) * REACH]
            halves[slot, 2 * b + 1 + u] = both[:, u * REACH : (u + 1) * REACH]

    def send_edges(step, slot):
        @pl.when(step < last)
        def _():
            for side in range(2):
                out_edge[step, side] = state[slot, tiles if side else 1]
                edge_copy(step, side).start()

    quarter = nodes // 4

    def seen(slot, t, f):
        at = place[t, pl.ds(f, 1), :]
        inner = at % REACH
        index = jnp.broadcast_to(inner, (nodes, REACH))
        tile = jnp.broadcast_to(at // REACH, (nodes, REACH))
        flip = signs[t, 0, pl.ds(f, 1), :]
        turn = signs[t, 1, pl.ds(f, 1), :]

        def take(k):
            return jnp.take_along_axis(
                state[slot, t + k], index, axis=1, mode="promise_in_bounds"
            )

        v = jnp.where(tile == 0, take(0), jnp.where(tile == 1, take(1), take(2)))
        return twisted(v, flip, turn)

    def twisted(v, flip, turn):
        return jnp.concatenate(
            [
                v[:quarter],
                v[quarter : 2 * quarter] * flip,
                v[2 * quarter : 3 * quarter] * turn,
                v[3 * quarter :] * (flip * turn),
            ],
            axis=0,
        )

    def seen_block(slot, b, p):
        window = jnp.concatenate([halves[slot, 2 * b + i] for i in range(4)], axis=1)
        v = jnp.dot(window, hot[b, p], preferred_element_type=F32)
        f = pl.ds(2 * p + 1, 1)
        flip, turn = [
            jnp.concatenate([signs[2 * b, i, f, :], signs[2 * b + 1, i, f, :]], axis=1)
            for i in range(2)
        ]
        return tuple(
            twisted(part, flip, turn).astype(BF16) for part in (v[:nodes], v[nodes:])
        )

    def apply(slot, b):
        own = jnp.concatenate([halves[slot, 2 * b + 1], halves[slot, 2 * b + 2]], axis=1)
        acc = jnp.dot(wide[FACES // 2], own, preferred_element_type=F32)
        rest = None
        for p in range(FACES // 2):
            parts = [
                split(
                    jnp.concatenate(
                        [seen(slot, 2 * b, 2 * p), seen(slot, 2 * b + 1, 2 * p)], axis=1
                    )
                ),
                seen_block(slot, b, p),
            ]
            high = jnp.concatenate([parts[0][0], parts[1][0]], axis=0)
            tail = jnp.concatenate([parts[0][1], parts[1][1]], axis=0)
            acc = acc + jnp.dot(wide[p], high, preferred_element_type=F32)
            more = jnp.dot(low[p], tail, preferred_element_type=F32)
            rest = more if rest is None else rest + more
        return acc[:nodes] + acc[nodes:] + rest

    for b in order:
        store(0, b, forcing(0, b))
    send_edges(0, 0)

    def advance(step, now):
        before = 1 - now
        for region in (order[:-2], order[-2:]):
            if region[0] == 0:
                for side in range(2):
                    edge_copy(step - 1, 1 - side).wait_recv()
                    edge = in_edge[step - 1, side]
                    state[before, (tiles + 1) * side] = edge
                    halves[before, (tiles + 1) * side] = jnp.concatenate(split(edge), axis=0)
            made = [apply(before, b) + forcing(step, b) for b in region]
            for b, y in zip(region, made):
                store(now, b, y)

            @pl.when(step < n)
            def _():
                for b in region:
                    arrive(step, b)
                    if square:

                        @pl.when(jnp.logical_and(n == 3, step == 1))
                        def _():
                            send(1, b, 2, False).start()

                    y = jnp.concatenate([state[now, 2 * b + 1], state[now, 2 * b + 2]], axis=1)
                    store(now, b, y + DIFF[STEPS] * coded[step, b])

        send_edges(step, now)
        for side in range(2):
            edge_copy(step - 1, side).wait_send()

    def two(i, carry):
        advance(2 * i + 1, 1)

        @pl.when(2 * i + 2 <= last)
        def _():
            advance(2 * i + 2, 0)

        return carry

    lax.fori_loop(0, (last + 1) // 2, two, 0)

    final = lax.rem(last, 2)
    turn_out = basis_t[...].astype(BF16)
    turn_out = jnp.concatenate([turn_out, turn_out], axis=0)

    for t in range(tiles):
        out[0, pl.ds(t * REACH, REACH), :] = jnp.dot(
            pair(jnp.transpose(state[final, t + 1])), turn_out, preferred_element_type=F32
        )

    if square:
        for who in range(times):

            @pl.when(n == who)
            def _():
                for hops, own in ((own_hops, True), (passed_hops, False)):
                    for sender, source, b, target in hops:
                        if sender == who:
                            send(source, b, target, own).wait_send()
    else:
        for target in range(1, times):

            @pl.when(n < target)
            def _():
                for b in order:
                    send(n, b, target, True).wait_send()


def solution(mesh):
    times, ring = mesh.shape["tm"], mesh.shape["space"]

    def per_device(starts, volume_op, face_lifts, neighbours, orientation):
        rows, nodes = starts.shape[1], starts.shape[2]
        blocks, tiles = rows // BLOCK, rows // REACH
        steps = times + STEPS
        basis_t = jnp.asarray(twist_basis(nodes).T.copy())
        return pl.pallas_call(
            functools.partial(kernel, times, ring),
            out_shape=jax.ShapeDtypeStruct(starts.shape, F32),
            in_specs=[pl.BlockSpec(memory_space=pltpu.VMEM)] * 6,
            out_specs=pl.BlockSpec(memory_space=pltpu.VMEM),
            scratch_shapes=[
                pltpu.VMEM((times, rows, nodes), F32),
                pltpu.VMEM((times, blocks, nodes, BLOCK), F32),
                pltpu.VMEM((2, tiles + 2, nodes, REACH), F32),
                pltpu.VMEM((2, tiles + 2, 2 * nodes, REACH), BF16),
                pltpu.VMEM((blocks, FACES // 2, WINDOW, BLOCK), BF16),
                pltpu.VMEM((tiles, FACES, REACH), jnp.int32),
                pltpu.VMEM((tiles, 2, FACES, REACH), F32),
                pltpu.VMEM((FACES // 2 + 1, 2 * nodes, 2 * nodes), BF16),
                pltpu.VMEM((FACES // 2, nodes, 2 * nodes), BF16),
                pltpu.VMEM((steps, 2, nodes, REACH), F32),
                pltpu.VMEM((steps, 2, nodes, REACH), F32),
                pltpu.SemaphoreType.DMA((times, times, blocks)),
                pltpu.SemaphoreType.DMA((times, blocks)),
                pltpu.SemaphoreType.DMA((steps, 2)),
                pltpu.SemaphoreType.DMA((steps, 2)),
            ],
            compiler_params=pltpu.CompilerParams(
                collective_id=0, has_side_effects=True, vmem_limit_bytes=50 * 1024 * 1024
            ),
        )(starts, volume_op, face_lifts, neighbours.T, orientation.T, basis_t)

    return jax.shard_map(
        per_device,
        mesh=mesh,
        in_specs=(P("tm", "space", None), P(), P(), P("space", None), P("space", None)),
        out_specs=P("tm", "space", None),
        check_vma=False,
    )
```

```python
import functools

import jax
import jax.numpy as jnp
import numpy as np
from jax import lax
from jax.experimental import pallas as pl
from jax.experimental.pallas import tpu as pltpu
from jax.sharding import PartitionSpec as P

REACH = 128
STEPS = 4
FACES = 6
PAIRS = FACES // 2

FINE = [81 / 256, 108 / 256, 54 / 256, 12 / 256, 1 / 256]
DIFF = [81 / 256, -148 / 256, 54 / 256, 12 / 256, 1 / 256]

MESH = pl.DeviceIdType.MESH
F32 = jnp.float32
BF16 = jnp.bfloat16


def twist_basis(nodes):
    quarter = nodes // 4
    basis = np.zeros((nodes, nodes), np.float32)
    for column in range(nodes):
        kind, rep = divmod(column, quarter)
        flip, turn = kind & 1, kind >> 1
        half = nodes // 2
        for a in range(2):
            for b in range(2):
                row = nodes - 1 - rep if a else rep
                row = (row + half) % nodes if b else row
                basis[row, column] = 0.5 * (-1) ** (flip * a + turn * b)
    return basis


def sizes(times, rows):
    tiles = rows // REACH
    longest = max(STEPS, times - 1)
    ghost = longest + longest % 2
    first = max(STEPS - 1, times - 2)
    depth = [STEPS, first] + [max(STEPS - 2, times - 2)] * (times - 2)
    if tiles > 2 * first:
        chunks = [(0, first), (tiles - first, first), (first, tiles - 2 * first)]
    else:
        chunks = [(0, tiles)]
    return tiles, longest, ghost, depth, chunks


def split(x):
    hi = x.astype(BF16)
    return hi, (x - hi.astype(F32)).astype(BF16)


def pair(x):
    return jnp.concatenate(split(x), axis=-1)


def kernel(
    times, ring, starts, volume_in, lifts_in, nbr_in, orient_in, basis_in, out,
    got, coded, state, halves, hot, place, signs, wide, low, out_edge, in_edge, first_end,
    volume, lifts, basis_t, nbr, orient,
    s_send, s_recv, g_send, g_recv, i_send, i_recv, u_send, u_recv, e_send, e_recv, here,
):
    rows, nodes = starts.shape[1], starts.shape[2]
    tiles, longest, ghost, depth, chunks = sizes(times, rows)
    n = lax.axis_index("tm")
    me = lax.axis_index("space")
    right, left = lax.rem(me + 1, ring), lax.rem(me + ring - 1, ring)
    square = times == 4

    def span(tile, count=1):
        return pl.ds((ghost + tile) * REACH, count * REACH)

    loads = [
        pltpu.make_async_copy(nbr_in, nbr.at[:, span(0, tiles)], here.at[0]),
        pltpu.make_async_copy(orient_in, orient.at[:, span(0, tiles)], here.at[1]),
        pltpu.make_async_copy(basis_in, basis_t, here.at[2]),
        pltpu.make_async_copy(lifts_in, lifts, here.at[3]),
        pltpu.make_async_copy(volume_in, volume, here.at[4]),
        pltpu.make_async_copy(starts.at[0], got.at[n, span(0, tiles)], here.at[5]),
    ]
    for copy in loads:
        copy.start()

    barrier = pltpu.get_barrier_semaphore()
    for side in (left, right):
        pl.semaphore_signal(barrier, inc=1, device_id={"space": side}, device_id_type=MESH)
    for step in range(1, times):
        pl.semaphore_signal(
            barrier, inc=1, device_id={"tm": lax.rem(n + step, times)}, device_id_type=MESH
        )
    pl.semaphore_wait(barrier, times + 1)

    def send(source, c, target, own):
        at, count = chunks[c]
        return pltpu.make_async_remote_copy(
            src_ref=starts.at[0, pl.ds(at * REACH, count * REACH)] if own else got.at[source, span(at, count)],
            dst_ref=got.at[source, span(at, count)],
            send_sem=s_send.at[target, source, c],
            recv_sem=s_recv.at[source, c],
            device_id={"tm": target},
            device_id_type=MESH,
        )

    def send_index(which, side):
        source = (nbr_in, orient_in)[which]
        held = (nbr, orient)[which]
        at = rows - ghost * REACH if side else 0
        return pltpu.make_async_remote_copy(
            src_ref=source.at[:, pl.ds(at, ghost * REACH)],
            dst_ref=held.at[:, span(-ghost if side else tiles, ghost)],
            send_sem=i_send.at[which, side],
            recv_sem=i_recv.at[which, 1 - side],
            device_id={"space": right if side else left},
            device_id_type=MESH,
        )

    def send_rim(source, side, i, own):
        tile = tiles - 1 - i if side else i
        return pltpu.make_async_remote_copy(
            src_ref=starts.at[0, pl.ds(tile * REACH, REACH)] if own else got.at[source, span(tile)],
            dst_ref=got.at[source, span(-1 - i if side else tiles + i)],
            send_sem=g_send.at[source, side, i],
            recv_sem=g_recv.at[source, 1 - side, i],
            device_id={"space": right if side else left},
            device_id_type=MESH,
        )

    def send_first(tile, target, own):
        return pltpu.make_async_remote_copy(
            src_ref=state.at[1, ghost + tile] if own else first_end.at[tile],
            dst_ref=first_end.at[tile],
            send_sem=u_send.at[target, tile],
            recv_sem=u_recv.at[tile],
            device_id={"tm": target},
            device_id_type=MESH,
        )

    def send_edge(side, i):
        return pltpu.make_async_remote_copy(
            src_ref=out_edge.at[side, i],
            dst_ref=in_edge.at[1 - side, i],
            send_sem=e_send.at[side, i],
            recv_sem=e_recv.at[1 - side, i],
            device_id={"space": right if side else left},
            device_id_type=MESH,
        )

    for which in range(2):
        for side in range(2):
            send_index(which, side).start()
    for who in range(times):

        @pl.when(n == who)
        def _():
            for i in range(depth[who]):
                for side in range(2):
                    send_rim(who, side, i, True).start()
            if who > 0:
                for c in range(len(chunks)):
                    for target in range(times - 1, who, -1):
                        if not (square and who == 1 and target == 2):
                            send(who, c, target, True).start()

    for copy in loads[2:5]:
        copy.wait()

    turn_in = basis_t[...].astype(BF16)
    turn_in = jnp.concatenate([turn_in, turn_in], axis=1)

    def rotate(x):
        return lax.dot_general(turn_in, pair(x), (((1,), (1,)), ((), ())), preferred_element_type=F32)

    def operator(a):
        return split(rotate(jnp.dot(turn_in, jnp.concatenate(split(a), axis=0), preferred_element_type=F32)))

    for p in range(PAIRS):
        h0, l0 = operator(lifts[2 * p])
        h1, l1 = operator(lifts[2 * p + 1])
        high = jnp.concatenate([h0, h1], axis=1)
        wide[p] = jnp.concatenate([high, jnp.concatenate([l0, l1], axis=1)], axis=0)
        low[p] = high
    hv, lv = operator(volume[...])
    wide[PAIRS] = jnp.concatenate(
        [jnp.concatenate([hv, hv], axis=1), jnp.concatenate([lv, lv], axis=1)], axis=0
    )

    rims = list(range(ghost)) + list(range(ghost + tiles, 2 * ghost + tiles))
    for slot in range(2):
        for t in rims:
            state[slot, t] = jnp.zeros((nodes, REACH), F32)
            halves[slot, t] = jnp.zeros((2 * nodes, REACH), BF16)
    for j in range(times):
        for t in rims:
            coded[j, t] = jnp.zeros((nodes, REACH), F32)

    total = rows * ring
    lane = lax.broadcasted_iota(jnp.int32, (FACES, REACH), 1)
    window = lax.broadcasted_iota(jnp.int32, (4 * REACH, 2 * REACH), 0)

    def locate(t):
        offset = nbr[:, span(t)] - (me * rows + t * REACH + lane)
        offset = jnp.where(offset > REACH, offset - total, offset)
        offset = jnp.where(offset < -REACH, offset + total, offset)
        place[ghost + t] = lane + REACH + offset
        o = orient[:, span(t)]
        signs[ghost + t, 0] = (1 - 2 * (o % 2)).astype(F32)
        signs[ghost + t, 1] = (1 - 2 * (o // 2)).astype(F32)

    def mark(t):
        for p in range(PAIRS):
            f = pl.ds(2 * p + 1, 1)
            row = jnp.concatenate([place[ghost + t, f, :], place[ghost + t + 1, f, :] + REACH], axis=1)
            hot[(ghost + t) // 2, p] = jnp.where(window == row, 1.0, 0.0).astype(BF16)

    def blocks(g):
        far = g + 1 - g % 2
        return list(range(-far, tiles + far, 2))

    inner = [t for t in blocks(0) if t >= 1 and t + 1 < tiles - 1]
    rim_blocks = [t for t in blocks(longest - 1) if t not in inner]

    for copy in loads[:2]:
        copy.wait()
    for t in range(tiles):
        locate(t)
    for t in inner:
        mark(t)

    def encode(j, tile, count):
        x = rotate(got[j, span(tile, count), :])
        for i in range(count):
            coded[j, ghost + tile + i] = x[:, i * REACH : (i + 1) * REACH]

    loads[5].wait()
    for at, count in chunks:
        encode(n, at, count)

    for c, (at, count) in enumerate(chunks):
        for j in range(1, times - 1):

            @pl.when(n > j)
            def _():
                send(j, c, n, False).wait_recv()
                for side in range(2):
                    for i in range(depth[j]):
                        tile = tiles - 1 - i if side else i
                        if at <= tile < at + count:
                            send_rim(j, side, i, False).start()
                if square and j == 1:

                    @pl.when(n == 3)
                    def _():
                        send(1, c, 2, False).start()

                encode(j, at, count)

    base = jnp.minimum(n, 1)

    def forcing(k, t):
        acc = None
        for i in range(STEPS + 1):
            j = base + k - STEPS + i
            held = jnp.logical_and(j >= base, j <= n)
            coef = jnp.where(n == 0, FINE[i], DIFF[i]).astype(F32)
            coef = jnp.where(held, coef, 0.0)
            j = jnp.where(held, j, base)
            both = jnp.concatenate([coded[j, ghost + t], coded[j, ghost + t + 1]], axis=1)
            acc = coef * both if acc is None else acc + coef * both
        return acc

    def put(slot, index, y):
        state[slot, index] = y
        halves[slot, index] = jnp.concatenate(split(y), axis=0)

    quarter = nodes // 4

    def twisted(v, flip, turn):
        return jnp.concatenate(
            [
                v[:quarter],
                v[quarter : 2 * quarter] * flip,
                v[2 * quarter : 3 * quarter] * turn,
                v[3 * quarter :] * (flip * turn),
            ],
            axis=0,
        )

    def seen(slot, t, f):
        at = place[t, pl.ds(f, 1), :]
        index = jnp.broadcast_to(at % REACH, (nodes, REACH))
        tile = jnp.broadcast_to(at // REACH, (nodes, REACH))

        def take(k):
            return jnp.take_along_axis(
                state[slot, t + k - 1], index, axis=1, mode="promise_in_bounds"
            )

        v = jnp.where(tile == 0, take(0), jnp.where(tile == 1, take(1), take(2)))
        return twisted(v, signs[t, 0, pl.ds(f, 1), :], signs[t, 1, pl.ds(f, 1), :])

    def seen_block(slot, t, p):
        view = jnp.concatenate([halves[slot, t - 1 + i] for i in range(4)], axis=1)
        v = jnp.dot(view, hot[t // 2, p], preferred_element_type=F32).astype(BF16)
        f = pl.ds(2 * p + 1, 1)
        flip, turn = [
            jnp.concatenate([signs[t, i, f, :], signs[t + 1, i, f, :]], axis=1).astype(BF16)
            for i in range(2)
        ]
        return twisted(v[:nodes], flip, turn), twisted(v[nodes:], flip, turn)

    def apply(slot, at, k):
        t = ghost + at
        seen_all = []
        for p in range(PAIRS):
            seen_all.append(
                (
                    split(jnp.concatenate([seen(slot, t, 2 * p), seen(slot, t + 1, 2 * p)], axis=1)),
                    seen_block(slot, t, p),
                )
            )
        own = jnp.concatenate([halves[slot, t], halves[slot, t + 1]], axis=1)
        acc = jnp.dot(wide[PAIRS], own, preferred_element_type=F32)
        rest = None
        for p, parts in enumerate(seen_all):
            high = jnp.concatenate([parts[0][0], parts[1][0]], axis=0)
            tail = jnp.concatenate([parts[0][1], parts[1][1]], axis=0)
            acc = acc + jnp.dot(wide[p], high, preferred_element_type=F32)
            more = jnp.dot(low[p], tail, preferred_element_type=F32)
            rest = more if rest is None else rest + more
        y = acc[:nodes] + acc[nodes:] + rest + forcing(k, at)
        for u in range(2):
            put(1 - slot, t + u, y[:, u * REACH : (u + 1) * REACH])

    start = jnp.where(n == 0, 1, 0)
    top = jnp.where(n == 0, FINE[STEPS], DIFF[STEPS]).astype(F32)
    for t in range(tiles):
        put(start, ghost + t, top * coded[base, ghost + t])

    half = tiles // 2

    def spread(tile, own):
        if square:

            @pl.when(jnp.logical_and(tile < half, n != 2))
            def _():
                send_first(tile, jnp.where(n == 0, 1, jnp.where(n == 1, 3, 2)), own).start()

            @pl.when(jnp.logical_and(tile >= half, n != 1))
            def _():
                send_first(tile, jnp.where(n == 0, 2, jnp.where(n == 2, 3, 1)), own).start()

        elif own:
            for target in range(times - 1, 0, -1):
                send_first(tile, target, True).start()

    def batch(phase, carry):
        need = jnp.where(phase == 0, jnp.where(n == 0, STEPS, STEPS - 1), n)
        since = jnp.where(phase == 0, 0, STEPS - 1)
        slot = lax.rem(need + 1, 2)

        @pl.when(phase == 1)
        def _():
            def body(i, carry):
                along = jnp.where(i < half, i, tiles - 1 + half - i)
                inward = jnp.where(i % 2 == 0, i // 2, tiles - 1 - i // 2)
                tile = jnp.where(n == 1, along, jnp.where(n == 2, tiles - 1 - along, inward))
                send_first(tile, n, False).wait_recv()
                spread(tile, False)
                z = state[1, ghost + tile] + first_end[tile]
                put(slot, ghost + tile, z)
                for side in range(2):
                    deep = tiles - 1 - tile if side else tile

                    @pl.when(deep < n)
                    def _():
                        out_edge[side, deep] = z
                        send_edge(side, deep).start()

                return carry

            lax.fori_loop(0, tiles, body, 0)

        for parity in range(2):

            @pl.when(slot == parity)
            def _():
                for t in inner:
                    apply(parity, t, since + 1)

        @pl.when(phase == 0)
        def _():
            for which in range(2):
                for side in range(2):
                    send_index(which, side).wait_recv()
            for t in range(-ghost, 0):
                locate(t)
                locate(tiles - 1 - t)
            for t in rim_blocks:
                mark(t)
            for j in range(times):

                @pl.when(jnp.logical_and(n >= j, (n == 0) == (j == 0)))
                def _():
                    for side in range(2):
                        for i in range(depth[j]):
                            send_rim(j, 1 - side, i, False).wait_recv()
                        encode(j, tiles if side else -depth[j], depth[j])

            for t in list(range(-depth[0], 0)) + list(range(tiles, tiles + depth[0])):
                put(start, ghost + t, top * coded[base, ghost + t])

        @pl.when(phase == 1)
        def _():
            for i in range(times - 1):

                @pl.when(i < n)
                def _():
                    for side in range(2):
                        send_edge(1 - side, i).wait_recv()
                        put(slot, ghost + tiles + i if side else ghost - 1 - i, in_edge[side, i])

        for g in range(longest - 1, -1, -1):

            @pl.when(need > g)
            def _():
                for t in blocks(g):
                    if t not in inner:
                        apply(g % 2, t, since + need - g)

            @pl.when(need - 1 > g)
            def _():
                for t in inner:
                    apply(g % 2, t, since + need - g)

        return carry

    lax.fori_loop(0, jnp.where(n == 0, 1, 2), batch, 0)

    @pl.when(n == 0)
    def _():
        for i in range(half):
            spread(i, True)
            spread(tiles - 1 - i, True)
        if tiles % 2:
            spread(half, True)

    turn_out = basis_t[...].astype(BF16)
    turn_out = jnp.concatenate([turn_out, turn_out], axis=0)
    for t in range(tiles):
        out[0, pl.ds(t * REACH, REACH), :] = jnp.dot(
            pair(jnp.transpose(state[1, ghost + t])), turn_out, preferred_element_type=F32
        )

    for which in range(2):
        for side in range(2):
            send_index(which, side).wait_send()
    for who in range(times):

        @pl.when(n == who)
        def _():
            for j in [0] if who == 0 else range(1, who + 1):
                for i in range(depth[j]):
                    for side in range(2):
                        send_rim(j, side, i, j == who).wait_send()
            if who > 0:
                for c in range(len(chunks)):
                    for target in range(who + 1, times):
                        if not (square and who == 1 and target == 2):
                            send(who, c, target, True).wait_send()
                    if square and who == 3:
                        send(1, c, 2, False).wait_send()
                for i in range(who):
                    for side in range(2):
                        send_edge(side, i).wait_send()
            for tile in range(tiles):
                if square:
                    hops = {0: 1, 1: 3, 3: 2} if tile < half else {0: 2, 2: 3, 3: 1}
                    targets = [hops[who]] if who in hops else []
                else:
                    targets = range(1, times) if who == 0 else []
                for target in targets:
                    send_first(tile, target, who == 0).wait_send()


def solution(mesh):
    times, ring = mesh.shape["tm"], mesh.shape["space"]

    def per_device(starts, volume_op, face_lifts, neighbours, orientation):
        rows, nodes = starts.shape[1], starts.shape[2]
        tiles, _, ghost, _, chunks = sizes(times, rows)
        held = tiles + 2 * ghost
        basis_t = jnp.asarray(twist_basis(nodes).T.copy())
        return pl.pallas_call(
            functools.partial(kernel, times, ring),
            out_shape=jax.ShapeDtypeStruct(starts.shape, F32),
            in_specs=[pl.BlockSpec(memory_space=pltpu.HBM)] * 6,
            out_specs=pl.BlockSpec(memory_space=pltpu.VMEM),
            scratch_shapes=[
                pltpu.VMEM((times, held * REACH, nodes), F32),
                pltpu.VMEM((times, held, nodes, REACH), F32),
                pltpu.VMEM((2, held, nodes, REACH), F32),
                pltpu.VMEM((2, held, 2 * nodes, REACH), BF16),
                pltpu.VMEM((held // 2, PAIRS, 4 * REACH, 2 * REACH), BF16),
                pltpu.VMEM((held, FACES, REACH), jnp.int32),
                pltpu.VMEM((held, 2, FACES, REACH), F32),
                pltpu.VMEM((PAIRS + 1, 2 * nodes, 2 * nodes), BF16),
                pltpu.VMEM((PAIRS, nodes, 2 * nodes), BF16),
                pltpu.VMEM((2, times - 1, nodes, REACH), F32),
                pltpu.VMEM((2, times - 1, nodes, REACH), F32),
                pltpu.VMEM((tiles, nodes, REACH), F32),
                pltpu.VMEM(volume_op.shape, F32),
                pltpu.VMEM(face_lifts.shape, F32),
                pltpu.VMEM((nodes, nodes), F32),
                pltpu.VMEM((FACES, held * REACH), jnp.int32),
                pltpu.VMEM((FACES, held * REACH), jnp.int32),
                pltpu.SemaphoreType.DMA((times, times, len(chunks))),
                pltpu.SemaphoreType.DMA((times, len(chunks))),
                pltpu.SemaphoreType.DMA((times, 2, ghost)),
                pltpu.SemaphoreType.DMA((times, 2, ghost)),
                pltpu.SemaphoreType.DMA((2, 2)),
                pltpu.SemaphoreType.DMA((2, 2)),
                pltpu.SemaphoreType.DMA((times, tiles)),
                pltpu.SemaphoreType.DMA((tiles,)),
                pltpu.SemaphoreType.DMA((2, times - 1)),
                pltpu.SemaphoreType.DMA((2, times - 1)),
                pltpu.SemaphoreType.DMA((6,)),
            ],
            compiler_params=pltpu.CompilerParams(
                collective_id=0, has_side_effects=True, vmem_limit_bytes=56 * 1024 * 1024
            ),
        )(starts, volume_op, face_lifts, neighbours.T, orientation.T, basis_t)

    return jax.shard_map(
        per_device,
        mesh=mesh,
        in_specs=(P("tm", "space", None), P(), P(), P("space", None), P("space", None)),
        out_specs=P("tm", "space", None),
        check_vma=False,
    )
```

```python
import functools

import jax
import jax.numpy as jnp
import numpy as np
from jax import lax
from jax.experimental import pallas as pl
from jax.experimental.pallas import tpu as pltpu
from jax.sharding import PartitionSpec as P

REACH = 128
STEPS = 4
FACES = 6
PAIRS = FACES // 2

FINE = [81 / 256, 108 / 256, 54 / 256, 12 / 256, 1 / 256]
DIFF = [81 / 256, -148 / 256, 54 / 256, 12 / 256, 1 / 256]

MESH = pl.DeviceIdType.MESH
F32 = jnp.float32
BF16 = jnp.bfloat16


def twist_basis(nodes):
    quarter = nodes // 4
    basis = np.zeros((nodes, nodes), np.float32)
    for column in range(nodes):
        kind, rep = divmod(column, quarter)
        flip, turn = kind & 1, kind >> 1
        half = nodes // 2
        for a in range(2):
            for b in range(2):
                row = nodes - 1 - rep if a else rep
                row = (row + half) % nodes if b else row
                basis[row, column] = 0.5 * (-1) ** (flip * a + turn * b)
    return basis


def sizes(times, rows):
    tiles = rows // REACH
    longest = max(STEPS, times - 1)
    ghost = longest + longest % 2
    first = max(STEPS - 1, times - 2)
    depth = [STEPS, first] + [max(STEPS - 2, times - 2)] * (times - 2)
    if tiles > 2 * first:
        chunks = [(0, first), (tiles - first, first), (first, tiles - 2 * first)]
    else:
        chunks = [(0, tiles)]
    return tiles, longest, ghost, depth, chunks


def split(x):
    hi = x.astype(BF16)
    return hi, (x - hi.astype(F32)).astype(BF16)


def pair(x):
    return jnp.concatenate(split(x), axis=-1)


def kernel(
    times, ring, starts, volume_in, lifts_in, nbr_in, orient_in, basis_in, out,
    got, coded, state, halves, hot, place, signs, wide, low, out_edge, in_edge, first_end,
    volume, lifts, basis_t, nbr, orient,
    s_send, s_recv, g_send, g_recv, i_send, i_recv, u_send, u_recv, e_send, e_recv, here,
):
    rows, nodes = starts.shape[1], starts.shape[2]
    tiles, longest, ghost, depth, chunks = sizes(times, rows)
    n = lax.axis_index("tm")
    me = lax.axis_index("space")
    right, left = lax.rem(me + 1, ring), lax.rem(me + ring - 1, ring)
    square = times == 4

    def span(tile, count=1):
        return pl.ds((ghost + tile) * REACH, count * REACH)

    loads = [
        pltpu.make_async_copy(nbr_in, nbr.at[:, span(0, tiles)], here.at[0]),
        pltpu.make_async_copy(orient_in, orient.at[:, span(0, tiles)], here.at[1]),
        pltpu.make_async_copy(basis_in, basis_t, here.at[2]),
        pltpu.make_async_copy(lifts_in, lifts, here.at[3]),
        pltpu.make_async_copy(volume_in, volume, here.at[4]),
        pltpu.make_async_copy(starts.at[0], got.at[n, span(0, tiles)], here.at[5]),
    ]
    for copy in loads:
        copy.start()

    barrier = pltpu.get_barrier_semaphore()
    for side in (left, right):
        pl.semaphore_signal(barrier, inc=1, device_id={"space": side}, device_id_type=MESH)
    for step in range(1, times):
        pl.semaphore_signal(
            barrier, inc=1, device_id={"tm": lax.rem(n + step, times)}, device_id_type=MESH
        )
    pl.semaphore_wait(barrier, times + 1)

    def send(source, c, target, own):
        at, count = chunks[c]
        return pltpu.make_async_remote_copy(
            src_ref=starts.at[0, pl.ds(at * REACH, count * REACH)] if own else got.at[source, span(at, count)],
            dst_ref=got.at[source, span(at, count)],
            send_sem=s_send.at[target, source, c],
            recv_sem=s_recv.at[source, c],
            device_id={"tm": target},
            device_id_type=MESH,
        )

    def send_index(which, side):
        source = (nbr_in, orient_in)[which]
        held = (nbr, orient)[which]
        at = rows - ghost * REACH if side else 0
        return pltpu.make_async_remote_copy(
            src_ref=source.at[:, pl.ds(at, ghost * REACH)],
            dst_ref=held.at[:, span(-ghost if side else tiles, ghost)],
            send_sem=i_send.at[which, side],
            recv_sem=i_recv.at[which, 1 - side],
            device_id={"space": right if side else left},
            device_id_type=MESH,
        )

    def send_rim(source, side, i, own):
        tile = tiles - 1 - i if side else i
        return pltpu.make_async_remote_copy(
            src_ref=starts.at[0, pl.ds(tile * REACH, REACH)] if own else got.at[source, span(tile)],
            dst_ref=got.at[source, span(-1 - i if side else tiles + i)],
            send_sem=g_send.at[source, side, i],
            recv_sem=g_recv.at[source, 1 - side, i],
            device_id={"space": right if side else left},
            device_id_type=MESH,
        )

    def send_first(tile, target, own):
        return pltpu.make_async_remote_copy(
            src_ref=state.at[1, ghost + tile] if own else first_end.at[tile],
            dst_ref=first_end.at[tile],
            send_sem=u_send.at[target, tile],
            recv_sem=u_recv.at[tile],
            device_id={"tm": target},
            device_id_type=MESH,
        )

    def send_edge(side, i):
        return pltpu.make_async_remote_copy(
            src_ref=out_edge.at[side, i],
            dst_ref=in_edge.at[1 - side, i],
            send_sem=e_send.at[side, i],
            recv_sem=e_recv.at[1 - side, i],
            device_id={"space": right if side else left},
            device_id_type=MESH,
        )

    for which in range(2):
        for side in range(2):
            send_index(which, side).start()
    for who in range(times):

        @pl.when(n == who)
        def _():
            for i in range(depth[who]):
                for side in range(2):
                    send_rim(who, side, i, True).start()
            if who > 0:
                for c in range(len(chunks)):
                    for target in range(times - 1, who, -1):
                        send(who, c, target, True).start()

    for copy in loads[2:5]:
        copy.wait()

    turn_in = basis_t[...].astype(BF16)
    turn_in = jnp.concatenate([turn_in, turn_in], axis=1)

    def rotate(x):
        return lax.dot_general(turn_in, pair(x), (((1,), (1,)), ((), ())), preferred_element_type=F32)

    def operator(a):
        return split(rotate(jnp.dot(turn_in, jnp.concatenate(split(a), axis=0), preferred_element_type=F32)))

    for p in range(PAIRS):
        h0, l0 = operator(lifts[2 * p])
        h1, l1 = operator(lifts[2 * p + 1])
        high = jnp.concatenate([h0, h1], axis=1)
        wide[p] = jnp.concatenate([high, jnp.concatenate([l0, l1], axis=1)], axis=0)
        low[p] = high
    hv, lv = operator(volume[...])
    wide[PAIRS] = jnp.concatenate(
        [jnp.concatenate([hv, hv], axis=1), jnp.concatenate([lv, lv], axis=1)], axis=0
    )

    rims = list(range(ghost)) + list(range(ghost + tiles, 2 * ghost + tiles))
    for slot in range(2):
        for t in rims:
            state[slot, t] = jnp.zeros((nodes, REACH), F32)
            halves[slot, t] = jnp.zeros((2 * nodes, REACH), BF16)
    for j in range(times):
        for t in rims:
            coded[j, t] = jnp.zeros((nodes, REACH), F32)

    total = rows * ring
    lane = lax.broadcasted_iota(jnp.int32, (FACES, REACH), 1)
    window = lax.broadcasted_iota(jnp.int32, (4 * REACH, 2 * REACH), 0)

    def locate(t):
        offset = nbr[:, span(t)] - (me * rows + t * REACH + lane)
        offset = jnp.where(offset > REACH, offset - total, offset)
        offset = jnp.where(offset < -REACH, offset + total, offset)
        place[ghost + t] = lane + REACH + offset
        o = orient[:, span(t)]
        signs[ghost + t, 0] = (1 - 2 * (o % 2)).astype(F32)
        signs[ghost + t, 1] = (1 - 2 * (o // 2)).astype(F32)

    def mark(t):
        for p in range(PAIRS):
            f = pl.ds(2 * p + 1, 1)
            row = jnp.concatenate([place[ghost + t, f, :], place[ghost + t + 1, f, :] + REACH], axis=1)
            hot[(ghost + t) // 2, p] = jnp.where(window == row, 1.0, 0.0).astype(BF16)

    def blocks(g):
        far = g + 1 - g % 2
        return list(range(-far, tiles + far, 2))

    inner = [t for t in blocks(0) if t >= 1 and t + 1 < tiles - 1]
    rim_blocks = [t for t in blocks(longest - 1) if t not in inner]

    for copy in loads[:2]:
        copy.wait()
    for t in range(tiles):
        locate(t)
    for t in inner:
        mark(t)

    def encode(j, tile, count):
        x = rotate(got[j, span(tile, count), :])
        for i in range(count):
            coded[j, ghost + tile + i] = x[:, i * REACH : (i + 1) * REACH]

    loads[5].wait()
    for at, count in chunks:
        encode(n, at, count)

    for c, (at, count) in enumerate(chunks):
        for j in range(1, times - 1):

            @pl.when(n > j)
            def _():
                send(j, c, n, False).wait_recv()
                for side in range(2):
                    for i in range(depth[j]):
                        tile = tiles - 1 - i if side else i
                        if at <= tile < at + count:
                            send_rim(j, side, i, False).start()
                encode(j, at, count)

    base = jnp.minimum(n, 1)

    def forcing(k, t):
        acc = None
        for i in range(STEPS + 1):
            j = base + k - STEPS + i
            held = jnp.logical_and(j >= base, j <= n)
            coef = jnp.where(n == 0, FINE[i], DIFF[i]).astype(F32)
            coef = jnp.where(held, coef, 0.0)
            j = jnp.where(held, j, base)
            both = jnp.concatenate([coded[j, ghost + t], coded[j, ghost + t + 1]], axis=1)
            acc = coef * both if acc is None else acc + coef * both
        return acc

    def put(slot, index, y):
        state[slot, index] = y
        halves[slot, index] = jnp.concatenate(split(y), axis=0)

    quarter = nodes // 4

    def twisted(v, flip, turn):
        return jnp.concatenate(
            [
                v[:quarter],
                v[quarter : 2 * quarter] * flip,
                v[2 * quarter : 3 * quarter] * turn,
                v[3 * quarter :] * (flip * turn),
            ],
            axis=0,
        )

    def seen(slot, t, f):
        at = place[t, pl.ds(f, 1), :]
        index = jnp.broadcast_to(at % REACH, (nodes, REACH))
        tile = jnp.broadcast_to(at // REACH, (nodes, REACH))

        def take(k):
            return jnp.take_along_axis(
                state[slot, t + k - 1], index, axis=1, mode="promise_in_bounds"
            )

        v = jnp.where(tile == 0, take(0), jnp.where(tile == 1, take(1), take(2)))
        return twisted(v, signs[t, 0, pl.ds(f, 1), :], signs[t, 1, pl.ds(f, 1), :])

    def seen_block(slot, t, p):
        view = jnp.concatenate([halves[slot, t - 1 + i] for i in range(4)], axis=1)
        v = jnp.dot(view, hot[t // 2, p], preferred_element_type=F32).astype(BF16)
        f = pl.ds(2 * p + 1, 1)
        flip, turn = [
            jnp.concatenate([signs[t, i, f, :], signs[t + 1, i, f, :]], axis=1).astype(BF16)
            for i in range(2)
        ]
        return twisted(v[:nodes], flip, turn), twisted(v[nodes:], flip, turn)

    def apply(slot, at, k):
        t = ghost + at
        seen_all = []
        for p in range(PAIRS):
            seen_all.append(
                (
                    split(jnp.concatenate([seen(slot, t, 2 * p), seen(slot, t + 1, 2 * p)], axis=1)),
                    seen_block(slot, t, p),
                )
            )
        own = jnp.concatenate([halves[slot, t], halves[slot, t + 1]], axis=1)
        acc = jnp.dot(wide[PAIRS], own, preferred_element_type=F32)
        rest = None
        for p, parts in enumerate(seen_all):
            high = jnp.concatenate([parts[0][0], parts[1][0]], axis=0)
            tail = jnp.concatenate([parts[0][1], parts[1][1]], axis=0)
            acc = acc + jnp.dot(wide[p], high, preferred_element_type=F32)
            more = jnp.dot(low[p], tail, preferred_element_type=F32)
            rest = more if rest is None else rest + more
        y = acc[:nodes] + acc[nodes:] + rest + forcing(k, at)
        for u in range(2):
            put(1 - slot, t + u, y[:, u * REACH : (u + 1) * REACH])

    start = jnp.where(n == 0, 1, 0)
    top = jnp.where(n == 0, FINE[STEPS], DIFF[STEPS]).astype(F32)
    for t in range(tiles):
        put(start, ghost + t, top * coded[base, ghost + t])

    half = tiles // 2

    def spread(tile, own):
        if square:

            @pl.when(jnp.logical_and(tile < half, n != 2))
            def _():
                send_first(tile, jnp.where(n == 0, 1, jnp.where(n == 1, 3, 2)), own).start()

            @pl.when(jnp.logical_and(tile >= half, n != 1))
            def _():
                send_first(tile, jnp.where(n == 0, 2, jnp.where(n == 2, 3, 1)), own).start()

        elif own:
            for target in range(times - 1, 0, -1):
                send_first(tile, target, True).start()

    def learn():
        for which in range(2):
            for side in range(2):
                send_index(which, side).wait_recv()
        for t in range(-ghost, 0):
            locate(t)
            locate(tiles - 1 - t)
        for t in rim_blocks:
            mark(t)

    def widen(j, at, count):
        for side in range(2):
            for i in range(at, at + count):
                send_rim(j, 1 - side, i, False).wait_recv()
            encode(j, tiles + at if side else -at - count, count)

    def begin(slot, at, count):
        for i in range(at, at + count):
            for t in (-1 - i, tiles + i):
                put(slot, ghost + t, top * coded[base, ghost + t])

    def batch(phase, carry):
        need = jnp.where(phase == 0, STEPS - 1, n)
        since = jnp.where(phase == 0, 0, STEPS - 1)
        slot = lax.rem(need + 1, 2)

        @pl.when(phase == 1)
        def _():
            def body(i, carry):
                along = jnp.where(i < half, i, tiles - 1 + half - i)
                inward = jnp.where(i % 2 == 0, i // 2, tiles - 1 - i // 2)
                tile = jnp.where(n == 1, along, jnp.where(n == 2, tiles - 1 - along, inward))
                send_first(tile, n, False).wait_recv()
                spread(tile, False)
                z = state[1, ghost + tile] + first_end[tile]
                put(slot, ghost + tile, z)
                for side in range(2):
                    deep = tiles - 1 - tile if side else tile

                    @pl.when(deep < n)
                    def _():
                        out_edge[side, deep] = z
                        send_edge(side, deep).start()

                return carry

            lax.fori_loop(0, tiles, body, 0)

        for parity in range(2):

            @pl.when(slot == parity)
            def _():
                for t in inner:
                    apply(parity, t, since + 1)

        @pl.when(phase == 0)
        def _():
            learn()
            for j in range(1, times):

                @pl.when(n >= j)
                def _():
                    widen(j, 0, depth[j])

            begin(0, 0, depth[1])

        @pl.when(phase == 1)
        def _():
            for i in range(times - 1):

                @pl.when(i < n)
                def _():
                    for side in range(2):
                        send_edge(1 - side, i).wait_recv()
                        put(slot, ghost + tiles + i if side else ghost - 1 - i, in_edge[side, i])

        for g in range(max(STEPS - 1, times - 1) - 1, -1, -1):

            @pl.when(need > g)
            def _():
                for t in blocks(g):
                    if t not in inner:
                        apply(g % 2, t, since + need - g)

            @pl.when(need - 1 > g)
            def _():
                for t in inner:
                    apply(g % 2, t, since + need - g)

        return carry

    @pl.when(n == 0)
    def _():
        rim = [-1, tiles - 1]
        outer = [-3, tiles + 1]
        core = inner[1:-1]
        wings = [t for t in inner if t not in core]
        for t in inner:
            apply(1, t, 1)
        learn()
        widen(0, 0, 2)
        begin(1, 0, 2)
        for slot, k, some in ((1, 1, rim), (0, 2, inner), (1, 3, core)):
            for t in some:
                apply(slot, t, k)
        widen(0, 2, STEPS - 2)
        begin(1, 2, STEPS - 2)
        for slot, k, some in ((1, 1, outer), (0, 2, outer + rim), (1, 3, rim + wings)):
            for t in some:
                apply(slot, t, k)
        for some in (rim, wings, core):
            for t in some:
                apply(0, t, STEPS)
            for t in some:
                for tile in (t, t + 1) if t < half - 1 else (t + 1, t):
                    if 0 <= tile < tiles:
                        spread(tile, True)

    lax.fori_loop(0, jnp.where(n == 0, 0, 2), batch, 0)

    turn_out = basis_t[...].astype(BF16)
    turn_out = jnp.concatenate([turn_out, turn_out], axis=0)
    for t in range(tiles):
        out[0, pl.ds(t * REACH, REACH), :] = jnp.dot(
            pair(jnp.transpose(state[1, ghost + t])), turn_out, preferred_element_type=F32
        )

    for which in range(2):
        for side in range(2):
            send_index(which, side).wait_send()
    for who in range(times):

        @pl.when(n == who)
        def _():
            for j in [0] if who == 0 else range(1, who + 1):
                for i in range(depth[j]):
                    for side in range(2):
                        send_rim(j, side, i, j == who).wait_send()
            if who > 0:
                for c in range(len(chunks)):
                    for target in range(who + 1, times):
                        send(who, c, target, True).wait_send()
                for i in range(who):
                    for side in range(2):
                        send_edge(side, i).wait_send()
            for tile in range(tiles):
                if square:
                    hops = {0: 1, 1: 3, 3: 2} if tile < half else {0: 2, 2: 3, 3: 1}
                    targets = [hops[who]] if who in hops else []
                else:
                    targets = range(1, times) if who == 0 else []
                for target in targets:
                    send_first(tile, target, who == 0).wait_send()


def solution(mesh):
    times, ring = mesh.shape["tm"], mesh.shape["space"]

    def per_device(starts, volume_op, face_lifts, neighbours, orientation):
        rows, nodes = starts.shape[1], starts.shape[2]
        tiles, _, ghost, _, chunks = sizes(times, rows)
        held = tiles + 2 * ghost
        basis_t = jnp.asarray(twist_basis(nodes).T.copy())
        return pl.pallas_call(
            functools.partial(kernel, times, ring),
            out_shape=jax.ShapeDtypeStruct(starts.shape, F32),
            in_specs=[pl.BlockSpec(memory_space=pltpu.HBM)] * 6,
            out_specs=pl.BlockSpec(memory_space=pltpu.VMEM),
            scratch_shapes=[
                pltpu.VMEM((times, held * REACH, nodes), F32),
                pltpu.VMEM((times, held, nodes, REACH), F32),
                pltpu.VMEM((2, held, nodes, REACH), F32),
                pltpu.VMEM((2, held, 2 * nodes, REACH), BF16),
                pltpu.VMEM((held // 2, PAIRS, 4 * REACH, 2 * REACH), BF16),
                pltpu.VMEM((held, FACES, REACH), jnp.int32),
                pltpu.VMEM((held, 2, FACES, REACH), F32),
                pltpu.VMEM((PAIRS + 1, 2 * nodes, 2 * nodes), BF16),
                pltpu.VMEM((PAIRS, nodes, 2 * nodes), BF16),
                pltpu.VMEM((2, times - 1, nodes, REACH), F32),
                pltpu.VMEM((2, times - 1, nodes, REACH), F32),
                pltpu.VMEM((tiles, nodes, REACH), F32),
                pltpu.VMEM(volume_op.shape, F32),
                pltpu.VMEM(face_lifts.shape, F32),
                pltpu.VMEM((nodes, nodes), F32),
                pltpu.VMEM((FACES, held * REACH), jnp.int32),
                pltpu.VMEM((FACES, held * REACH), jnp.int32),
                pltpu.SemaphoreType.DMA((times, times, len(chunks))),
                pltpu.SemaphoreType.DMA((times, len(chunks))),
                pltpu.SemaphoreType.DMA((times, 2, ghost)),
                pltpu.SemaphoreType.DMA((times, 2, ghost)),
                pltpu.SemaphoreType.DMA((2, 2)),
                pltpu.SemaphoreType.DMA((2, 2)),
                pltpu.SemaphoreType.DMA((times, tiles)),
                pltpu.SemaphoreType.DMA((tiles,)),
                pltpu.SemaphoreType.DMA((2, times - 1)),
                pltpu.SemaphoreType.DMA((2, times - 1)),
                pltpu.SemaphoreType.DMA((6,)),
            ],
            compiler_params=pltpu.CompilerParams(
                collective_id=0, has_side_effects=True, vmem_limit_bytes=56 * 1024 * 1024
            ),
        )(starts, volume_op, face_lifts, neighbours.T, orientation.T, basis_t)

    return jax.shard_map(
        per_device,
        mesh=mesh,
        in_specs=(P("tm", "space", None), P(), P(), P("space", None), P("space", None)),
        out_specs=P("tm", "space", None),
        check_vma=False,
    )
```

```python
import functools

import jax
import jax.numpy as jnp
import numpy as np
from jax import lax
from jax.experimental import pallas as pl
from jax.experimental.pallas import tpu as pltpu
from jax.sharding import PartitionSpec as P

REACH = 128
STEPS = 4
FACES = 6
PAIRS = FACES // 2

FINE = [81 / 256, 108 / 256, 54 / 256, 12 / 256, 1 / 256]
DIFF = [81 / 256, -148 / 256, 54 / 256, 12 / 256, 1 / 256]

MESH = pl.DeviceIdType.MESH
F32 = jnp.float32
BF16 = jnp.bfloat16


def twist_basis(nodes):
    quarter = nodes // 4
    basis = np.zeros((nodes, nodes), np.float32)
    for column in range(nodes):
        kind, rep = divmod(column, quarter)
        flip, turn = kind & 1, kind >> 1
        half = nodes // 2
        for a in range(2):
            for b in range(2):
                row = nodes - 1 - rep if a else rep
                row = (row + half) % nodes if b else row
                basis[row, column] = 0.5 * (-1) ** (flip * a + turn * b)
    return basis


def sizes(times, rows):
    tiles = rows // REACH
    longest = max(STEPS, times - 1)
    ghost = longest + longest % 2
    first = max(STEPS - 1, times - 2)
    depth = [STEPS, first] + [max(STEPS - 2, times - 2)] * (times - 2)
    if tiles > 2 * first:
        chunks = [(0, first), (tiles - first, first), (first, tiles - 2 * first)]
    else:
        chunks = [(0, tiles)]
    return tiles, longest, ghost, depth, chunks


def blocks(g, tiles):
    return list(range(-g, tiles + g, 2))


def spots(longest, tiles):
    starts = sorted({t for g in range(longest) for t in blocks(g, tiles)})
    return {t: i for i, t in enumerate(starts)}


def split(x):
    hi = x.astype(BF16)
    return hi, (x - hi.astype(F32)).astype(BF16)


def pair(x):
    return jnp.concatenate(split(x), axis=-1)


def kernel(
    times, ring, starts, volume_in, lifts_in, nbr_in, orient_in, basis_in, out,
    got, coded, state, halves, hot, place, signs, wide, low, out_edge, in_edge, first_end,
    volume, lifts, basis_t, nbr, orient,
    s_send, s_recv, g_send, g_recv, i_send, i_recv, u_send, u_recv, e_send, e_recv, here,
):
    rows, nodes = starts.shape[1], starts.shape[2]
    tiles, longest, ghost, depth, chunks = sizes(times, rows)
    n = lax.axis_index("tm")
    me = lax.axis_index("space")
    right, left = lax.rem(me + 1, ring), lax.rem(me + ring - 1, ring)
    square = times == 4

    def span(tile, count=1):
        return pl.ds((ghost + tile) * REACH, count * REACH)

    loads = [
        pltpu.make_async_copy(nbr_in, nbr.at[:, span(0, tiles)], here.at[0]),
        pltpu.make_async_copy(orient_in, orient.at[:, span(0, tiles)], here.at[1]),
        pltpu.make_async_copy(basis_in, basis_t, here.at[2]),
        pltpu.make_async_copy(lifts_in, lifts, here.at[3]),
        pltpu.make_async_copy(volume_in, volume, here.at[4]),
        pltpu.make_async_copy(starts.at[0], got.at[n, span(0, tiles)], here.at[5]),
    ]
    for copy in loads:
        copy.start()

    barrier = pltpu.get_barrier_semaphore()
    for side in (left, right):
        pl.semaphore_signal(barrier, inc=1, device_id={"space": side}, device_id_type=MESH)
    for step in range(1, times):
        pl.semaphore_signal(
            barrier, inc=1, device_id={"tm": lax.rem(n + step, times)}, device_id_type=MESH
        )
    pl.semaphore_wait(barrier, times + 1)

    def send(source, c, target, own):
        at, count = chunks[c]
        return pltpu.make_async_remote_copy(
            src_ref=starts.at[0, pl.ds(at * REACH, count * REACH)] if own else got.at[source, span(at, count)],
            dst_ref=got.at[source, span(at, count)],
            send_sem=s_send.at[target, source, c],
            recv_sem=s_recv.at[source, c],
            device_id={"tm": target},
            device_id_type=MESH,
        )

    def send_index(which, side):
        source = (nbr_in, orient_in)[which]
        held = (nbr, orient)[which]
        at = rows - ghost * REACH if side else 0
        return pltpu.make_async_remote_copy(
            src_ref=source.at[:, pl.ds(at, ghost * REACH)],
            dst_ref=held.at[:, span(-ghost if side else tiles, ghost)],
            send_sem=i_send.at[which, side],
            recv_sem=i_recv.at[which, 1 - side],
            device_id={"space": right if side else left},
            device_id_type=MESH,
        )

    def send_rim(source, side, i, own):
        tile = tiles - 1 - i if side else i
        return pltpu.make_async_remote_copy(
            src_ref=starts.at[0, pl.ds(tile * REACH, REACH)] if own else got.at[source, span(tile)],
            dst_ref=got.at[source, span(-1 - i if side else tiles + i)],
            send_sem=g_send.at[source, side, i],
            recv_sem=g_recv.at[source, 1 - side, i],
            device_id={"space": right if side else left},
            device_id_type=MESH,
        )

    def send_first(tile, target, own):
        return pltpu.make_async_remote_copy(
            src_ref=state.at[1, ghost + tile] if own else first_end.at[tile],
            dst_ref=first_end.at[tile],
            send_sem=u_send.at[target, tile],
            recv_sem=u_recv.at[tile],
            device_id={"tm": target},
            device_id_type=MESH,
        )

    def send_edge(side, i):
        return pltpu.make_async_remote_copy(
            src_ref=out_edge.at[side, i],
            dst_ref=in_edge.at[1 - side, i],
            send_sem=e_send.at[side, i],
            recv_sem=e_recv.at[1 - side, i],
            device_id={"space": right if side else left},
            device_id_type=MESH,
        )

    for which in range(2):
        for side in range(2):
            send_index(which, side).start()
    for who in range(times):

        @pl.when(n == who)
        def _():
            for i in range(depth[who]):
                for side in range(2):
                    send_rim(who, side, i, True).start()
            if who > 0:
                for c in range(len(chunks)):
                    for target in range(times - 1, who, -1):
                        send(who, c, target, True).start()

    for copy in loads[2:5]:
        copy.wait()

    turn_in = basis_t[...].astype(BF16)
    turn_in = jnp.concatenate([turn_in, turn_in], axis=1)

    def rotate(x):
        return lax.dot_general(turn_in, pair(x), (((1,), (1,)), ((), ())), preferred_element_type=F32)

    def operator(a):
        return split(rotate(jnp.dot(turn_in, jnp.concatenate(split(a), axis=0), preferred_element_type=F32)))

    for p in range(PAIRS):
        h0, l0 = operator(lifts[2 * p])
        h1, l1 = operator(lifts[2 * p + 1])
        high = jnp.concatenate([h0, h1], axis=1)
        wide[p] = jnp.concatenate([high, jnp.concatenate([l0, l1], axis=1)], axis=0)
        low[p] = high
    hv, lv = operator(volume[...])
    wide[PAIRS] = jnp.concatenate(
        [jnp.concatenate([hv, hv], axis=1), jnp.concatenate([lv, lv], axis=1)], axis=0
    )

    rims = list(range(ghost)) + list(range(ghost + tiles, 2 * ghost + tiles))
    for slot in range(2):
        for t in rims:
            state[slot, t] = jnp.zeros((nodes, REACH), F32)
            halves[slot, t] = jnp.zeros((2 * nodes, REACH), BF16)
    for j in range(times):
        for t in rims:
            coded[j, t] = jnp.zeros((nodes, REACH), F32)

    total = rows * ring
    lane = lax.broadcasted_iota(jnp.int32, (FACES, REACH), 1)
    window = lax.broadcasted_iota(jnp.int32, (4 * REACH, 2 * REACH), 0)

    def locate(t):
        offset = nbr[:, span(t)] - (me * rows + t * REACH + lane)
        offset = jnp.where(offset > REACH, offset - total, offset)
        offset = jnp.where(offset < -REACH, offset + total, offset)
        place[ghost + t] = lane + REACH + offset
        o = orient[:, span(t)]
        signs[ghost + t, 0] = (1 - 2 * (o % 2)).astype(F32)
        signs[ghost + t, 1] = (1 - 2 * (o // 2)).astype(F32)

    def mark(t):
        for p in range(PAIRS):
            f = pl.ds(2 * p + 1, 1)
            row = jnp.concatenate([place[ghost + t, f, :], place[ghost + t + 1, f, :] + REACH], axis=1)
            hot[where[t], p] = jnp.where(window == row, 1.0, 0.0).astype(BF16)

    def inner(g):
        return [t for t in blocks(g, tiles) if t >= 1 and t + 1 < tiles - 1]

    where = spots(longest, tiles)
    own_blocks = [t for t in where if t >= 0 and t + 1 < tiles]
    rim_blocks = [t for t in where if t not in own_blocks]

    for copy in loads[:2]:
        copy.wait()
    for t in range(tiles):
        locate(t)
    for t in own_blocks:
        mark(t)

    def encode(j, tile, count):
        x = rotate(got[j, span(tile, count), :])
        for i in range(count):
            coded[j, ghost + tile + i] = x[:, i * REACH : (i + 1) * REACH]

    loads[5].wait()
    for at, count in chunks:
        encode(n, at, count)

    for c, (at, count) in enumerate(chunks):
        for j in range(1, times - 1):

            @pl.when(n > j)
            def _():
                send(j, c, n, False).wait_recv()
                for side in range(2):
                    for i in range(depth[j]):
                        tile = tiles - 1 - i if side else i
                        if at <= tile < at + count:
                            send_rim(j, side, i, False).start()
                encode(j, at, count)

    base = jnp.minimum(n, 1)

    def forcing(k, t):
        acc = None
        for i in range(STEPS + 1):
            j = base + k - STEPS + i
            held = jnp.logical_and(j >= base, j <= n)
            coef = jnp.where(n == 0, FINE[i], DIFF[i]).astype(F32)
            coef = jnp.where(held, coef, 0.0)
            j = jnp.where(held, j, base)
            both = jnp.concatenate([coded[j, ghost + t], coded[j, ghost + t + 1]], axis=1)
            acc = coef * both if acc is None else acc + coef * both
        return acc

    def put(slot, index, y):
        state[slot, index] = y
        halves[slot, index] = jnp.concatenate(split(y), axis=0)

    quarter = nodes // 4

    def twisted(v, flip, turn):
        return jnp.concatenate(
            [
                v[:quarter],
                v[quarter : 2 * quarter] * flip,
                v[2 * quarter : 3 * quarter] * turn,
                v[3 * quarter :] * (flip * turn),
            ],
            axis=0,
        )

    def seen(slot, t, f):
        at = place[t, pl.ds(f, 1), :]
        index = jnp.broadcast_to(at % REACH, (nodes, REACH))
        tile = jnp.broadcast_to(at // REACH, (nodes, REACH))

        def take(k):
            return jnp.take_along_axis(
                state[slot, t + k - 1], index, axis=1, mode="promise_in_bounds"
            )

        v = jnp.where(tile == 0, take(0), jnp.where(tile == 1, take(1), take(2)))
        return twisted(v, signs[t, 0, pl.ds(f, 1), :], signs[t, 1, pl.ds(f, 1), :])

    def seen_block(slot, t, p, spot):
        view = jnp.concatenate([halves[slot, t - 1 + i] for i in range(4)], axis=1)
        v = jnp.dot(view, hot[spot, p], preferred_element_type=F32).astype(BF16)
        f = pl.ds(2 * p + 1, 1)
        flip, turn = [
            jnp.concatenate([signs[t, i, f, :], signs[t + 1, i, f, :]], axis=1).astype(BF16)
            for i in range(2)
        ]
        return twisted(v[:nodes], flip, turn), twisted(v[nodes:], flip, turn)

    def apply(slot, at, k):
        t = ghost + at
        seen_all = []
        for p in range(PAIRS):
            seen_all.append(
                (
                    split(jnp.concatenate([seen(slot, t, 2 * p), seen(slot, t + 1, 2 * p)], axis=1)),
                    seen_block(slot, t, p, where[at]),
                )
            )
        own = jnp.concatenate([halves[slot, t], halves[slot, t + 1]], axis=1)
        acc = jnp.dot(wide[PAIRS], own, preferred_element_type=F32)
        rest = None
        for p, parts in enumerate(seen_all):
            high = jnp.concatenate([parts[0][0], parts[1][0]], axis=0)
            tail = jnp.concatenate([parts[0][1], parts[1][1]], axis=0)
            acc = acc + jnp.dot(wide[p], high, preferred_element_type=F32)
            more = jnp.dot(low[p], tail, preferred_element_type=F32)
            rest = more if rest is None else rest + more
        y = acc[:nodes] + acc[nodes:] + rest + forcing(k, at)
        for u in range(2):
            put(1 - slot, t + u, y[:, u * REACH : (u + 1) * REACH])

    start = jnp.where(n == 0, 1, 0)
    top = jnp.where(n == 0, FINE[STEPS], DIFF[STEPS]).astype(F32)
    for t in range(tiles):
        put(start, ghost + t, top * coded[base, ghost + t])

    half = tiles // 2

    def spread(tile, own):
        if square:

            @pl.when(jnp.logical_and(tile < half, n != 2))
            def _():
                send_first(tile, jnp.where(n == 0, 1, jnp.where(n == 1, 3, 2)), own).start()

            @pl.when(jnp.logical_and(tile >= half, n != 1))
            def _():
                send_first(tile, jnp.where(n == 0, 2, jnp.where(n == 2, 3, 1)), own).start()

        elif own:
            for target in range(times - 1, 0, -1):
                send_first(tile, target, True).start()

    def learn():
        for which in range(2):
            for side in range(2):
                send_index(which, side).wait_recv()
        for t in range(-ghost, 0):
            locate(t)
            locate(tiles - 1 - t)
        for t in rim_blocks:
            mark(t)

    def widen(j, at, count):
        for side in range(2):
            for i in range(at, at + count):
                send_rim(j, 1 - side, i, False).wait_recv()
            encode(j, tiles + at if side else -at - count, count)

    def begin(slot, at, count):
        for i in range(at, at + count):
            for t in (-1 - i, tiles + i):
                put(slot, ghost + t, top * coded[base, ghost + t])

    def turn(i):
        return (i + half // 2) % half

    def relay(tile):
        send_first(tile, n, False).wait_recv()
        spread(tile, False)

    def batch(phase, carry):
        need = jnp.where(phase == 0, STEPS - 1, n)
        since = jnp.where(phase == 0, 0, STEPS - 1)
        slot = lax.rem(need + 1, 2)

        @pl.when(phase == 1)
        def _():
            def body(i, carry):
                along = jnp.where(i < half, turn(i), tiles - 1 - turn(i - half))
                inward = jnp.where(i % 2 == 0, turn(i // 2), tiles - 1 - turn(i // 2))
                tile = jnp.where(n == 1, along, jnp.where(n == 2, tiles - 1 - along, inward))
                early = jnp.logical_and(n == 3, jnp.logical_and(tile >= half // 2, tile < half))
                early = jnp.logical_or(early, jnp.logical_and(n == 2, tile >= half))

                @pl.when(jnp.logical_not(jnp.logical_and(early, square)))
                def _():
                    relay(tile)

                z = state[1, ghost + tile] + first_end[tile]
                put(slot, ghost + tile, z)
                for side in range(2):
                    deep = tiles - 1 - tile if side else tile

                    @pl.when(deep < n)
                    def _():
                        out_edge[side, deep] = z
                        send_edge(side, deep).start()

                return carry

            lax.fori_loop(0, tiles, body, 0)

        for parity in range(2):

            @pl.when(slot == parity)
            def _():
                for t in inner(parity):
                    apply(parity, t, since + 1)

        @pl.when(phase == 0)
        def _():
            learn()
            for j in range(1, times):

                @pl.when(n >= j)
                def _():
                    widen(j, 0, depth[j])

            begin(0, 0, depth[1])

        @pl.when(phase == 1)
        def _():
            for i in range(times - 1):

                @pl.when(i < n)
                def _():
                    for side in range(2):
                        send_edge(1 - side, i).wait_recv()
                        put(slot, ghost + tiles + i if side else ghost - 1 - i, in_edge[side, i])

        for g in range(max(STEPS - 1, times - 1) - 1, -1, -1):

            @pl.when(need > g)
            def _():
                for t in blocks(g, tiles):
                    if t not in inner(g):
                        apply(g % 2, t, since + need - g)

            @pl.when(need - 1 > g)
            def _():
                for t in inner(g):
                    apply(g % 2, t, since + need - g)

            if square and g in (1, 2):

                @pl.when(jnp.logical_and(phase == 0, n == 2))
                def _():
                    for i in range((2 - g) * half // 2, (3 - g) * half // 2):
                        relay(tiles - 1 - turn(i))

            if square and g == 1:

                @pl.when(jnp.logical_and(phase == 0, n == 3))
                def _():
                    for i in range(half // 2):
                        relay(turn(i))

        return carry

    @pl.when(n == 0)
    def _():
        def advance(steps):
            for k in range(1, STEPS + 1):
                for t in steps[k - 1]:
                    apply((STEPS - k) % 2, t, k)

        near = [[t for t in blocks(STEPS - k, tiles) if k - 3 <= t and t + 1 <= tiles + 2 - k] for k in range(1, STEPS + 1)]
        for t in inner(STEPS - 1):
            apply(1, t, 1)
        learn()
        widen(0, 0, 2)
        begin(1, 0, 2)
        advance([[t for t in near[0] if t not in inner(STEPS - 1)]] + near[1:])
        for i in range(half // 2):
            spread(turn(i), True)
            spread(tiles - 1 - turn(i), True)
        widen(0, 2, STEPS - 2)
        begin(1, 2, STEPS - 2)
        advance([[t for t in blocks(STEPS - k, tiles) if t not in near[k - 1]] for k in range(1, STEPS + 1)])
        for i in range(half // 2, half):
            spread(turn(i), True)
            spread(tiles - 1 - turn(i), True)

    lax.fori_loop(0, jnp.where(n == 0, 0, 2), batch, 0)

    turn_out = basis_t[...].astype(BF16)
    turn_out = jnp.concatenate([turn_out, turn_out], axis=0)
    for t in range(tiles):
        out[0, pl.ds(t * REACH, REACH), :] = jnp.dot(
            pair(jnp.transpose(state[1, ghost + t])), turn_out, preferred_element_type=F32
        )

    for which in range(2):
        for side in range(2):
            send_index(which, side).wait_send()
    for who in range(times):

        @pl.when(n == who)
        def _():
            for j in [0] if who == 0 else range(1, who + 1):
                for i in range(depth[j]):
                    for side in range(2):
                        send_rim(j, side, i, j == who).wait_send()
            if who > 0:
                for c in range(len(chunks)):
                    for target in range(who + 1, times):
                        send(who, c, target, True).wait_send()
                for i in range(who):
                    for side in range(2):
                        send_edge(side, i).wait_send()
            for tile in range(tiles):
                if square:
                    hops = {0: 1, 1: 3, 3: 2} if tile < half else {0: 2, 2: 3, 3: 1}
                    targets = [hops[who]] if who in hops else []
                else:
                    targets = range(1, times) if who == 0 else []
                for target in targets:
                    send_first(tile, target, who == 0).wait_send()


def solution(mesh):
    times, ring = mesh.shape["tm"], mesh.shape["space"]

    def per_device(starts, volume_op, face_lifts, neighbours, orientation):
        rows, nodes = starts.shape[1], starts.shape[2]
        tiles, longest, ghost, _, chunks = sizes(times, rows)
        held = tiles + 2 * ghost
        basis_t = jnp.asarray(twist_basis(nodes).T.copy())
        return pl.pallas_call(
            functools.partial(kernel, times, ring),
            out_shape=jax.ShapeDtypeStruct(starts.shape, F32),
            in_specs=[pl.BlockSpec(memory_space=pltpu.HBM)] * 6,
            out_specs=pl.BlockSpec(memory_space=pltpu.VMEM),
            scratch_shapes=[
                pltpu.VMEM((times, held * REACH, nodes), F32),
                pltpu.VMEM((times, held, nodes, REACH), F32),
                pltpu.VMEM((2, held, nodes, REACH), F32),
                pltpu.VMEM((2, held, 2 * nodes, REACH), BF16),
                pltpu.VMEM((len(spots(longest, tiles)), PAIRS, 4 * REACH, 2 * REACH), BF16),
                pltpu.VMEM((held, FACES, REACH), jnp.int32),
                pltpu.VMEM((held, 2, FACES, REACH), F32),
                pltpu.VMEM((PAIRS + 1, 2 * nodes, 2 * nodes), BF16),
                pltpu.VMEM((PAIRS, nodes, 2 * nodes), BF16),
                pltpu.VMEM((2, times - 1, nodes, REACH), F32),
                pltpu.VMEM((2, times - 1, nodes, REACH), F32),
                pltpu.VMEM((tiles, nodes, REACH), F32),
                pltpu.VMEM(volume_op.shape, F32),
                pltpu.VMEM(face_lifts.shape, F32),
                pltpu.VMEM((nodes, nodes), F32),
                pltpu.VMEM((FACES, held * REACH), jnp.int32),
                pltpu.VMEM((FACES, held * REACH), jnp.int32),
                pltpu.SemaphoreType.DMA((times, times, len(chunks))),
                pltpu.SemaphoreType.DMA((times, len(chunks))),
                pltpu.SemaphoreType.DMA((times, 2, ghost)),
                pltpu.SemaphoreType.DMA((times, 2, ghost)),
                pltpu.SemaphoreType.DMA((2, 2)),
                pltpu.SemaphoreType.DMA((2, 2)),
                pltpu.SemaphoreType.DMA((times, tiles)),
                pltpu.SemaphoreType.DMA((tiles,)),
                pltpu.SemaphoreType.DMA((2, times - 1)),
                pltpu.SemaphoreType.DMA((2, times - 1)),
                pltpu.SemaphoreType.DMA((6,)),
            ],
            compiler_params=pltpu.CompilerParams(
                collective_id=0, has_side_effects=True, vmem_limit_bytes=56 * 1024 * 1024
            ),
        )(starts, volume_op, face_lifts, neighbours.T, orientation.T, basis_t)

    return jax.shard_map(
        per_device,
        mesh=mesh,
        in_specs=(P("tm", "space", None), P(), P(), P("space", None), P("space", None)),
        out_specs=P("tm", "space", None),
        check_vma=False,
    )
```
